32 devices in a mesh: seq: 8 (over z, y), col: 4 (over x, core).
Axes of the slice: x: 2, y: 2, z: 4, core: 2. Of those that a mesh axis runs over, the one named last changes fastest.
Arguments:
- activations: bfloat16 [8192, 3584], P('seq', 'col'), may hold values from -60 to 60
- start_basis: bfloat16 [3584, 512], P('col'), may hold values from -6 to 6
- gradient: bfloat16 [3584, 3584], P(None, ('seq', 'col')), may hold values from -12 to 12
Outputs:
- projected: bfloat16 [3584, 3584], P(None, ('seq', 'col'))
The draws below stay inside these ranges and needn't reach their ends.
All inputs are finite; a program needn't handle non-finite values.
Results may differ from the reference program's by a relative error of at most 0.019.
Values may be sent and summed in bfloat16 or wider, within the bound.
No kernel may reach another device: no remote copies, remote signals or barrier semaphores. Data moves between devices by JAX's collectives and lax.ppermute only.
A program may use at most 64 MiB of HBM per device.

```python
import jax
import jax.numpy as jnp
from jax import lax

D = 3584
DOUT = 3584
K = 512
ITERS = 2
TOKENS = 8192
N_COL = 4


def feature_scales(key):
    return jnp.exp(jax.random.uniform(jax.random.fold_in(key, 7), (D, 1), jnp.float32, jnp.log(0.4), jnp.log(2.5)))


def draw_activations(key, part):
    noise_key = jax.random.fold_in(key, 11)
    row_key = jax.random.fold_in(key, 13)
    values = jnp.clip(jax.random.normal(noise_key, (TOKENS, D), jnp.float32), -4.0, 4.0)
    row_scale = jnp.exp(jax.random.uniform(row_key, (TOKENS, 1), jnp.float32, jnp.log(0.5), jnp.log(2.0)))
    token_ramp = jnp.exp(0.55 * jnp.arange(TOKENS, dtype=jnp.float32)[:, None] / TOKENS)
    scaled = values * row_scale * token_ramp * feature_scales(key).T
    return jnp.clip(scaled, -60.0, 60.0).astype(jnp.bfloat16)


def draw_gradient(key, part):
    noise_key = jax.random.fold_in(key, 19)
    values = jnp.clip(jax.random.normal(noise_key, (D, DOUT), jnp.float32), -4.0, 4.0)
    return jnp.clip(values * feature_scales(key), -12.0, 12.0).astype(jnp.bfloat16)


def levels(rng, extent, shards, smallest, top_value):
    level = 1.0
    for position, parts in shards:
        draws = jax.random.uniform(jax.random.fold_in(jax.random.fold_in(rng, 6), position), (parts,), jnp.float32, smallest / len(shards), top_value / len(shards))
        level = level * jnp.repeat(jnp.exp(draws), extent[position] // parts).reshape((-1,) + (1,) * (len(extent) - 1 - position))
    return level


def scatter_about(rng, shape, width, limit, shards=(), held_as=jnp.bfloat16):
    array = width * jax.random.normal(rng, shape, jnp.float32)
    if shards:
        array = array * levels(rng, shape, shards, -0.22, 0.18)
    return jnp.clip(array, -limit, limit).astype(held_as)


def setup_inputs(seed: int = 0) -> dict:
    seeds = jax.random.split(jax.random.key(seed), 4)
    activations = draw_activations(jax.random.fold_in(seeds[3], 71), 0)
    start_basis = scatter_about(seeds[1], (D, K), 1.0, 6.0, ((0, 4),))
    gradient = draw_gradient(jax.random.fold_in(seeds[3], 71), 0)
    return {"activations": activations, "start_basis": start_basis, "gradient": gradient}


def contract_rows(left, right):
    return lax.dot_general(left.astype(jnp.float32), right.astype(jnp.float32), (((0,), (0,)), ((), ())), preferred_element_type=jnp.float32)

def reference(activations, start_basis, gradient):
    quarter = D // N_COL
    basis_now = start_basis
    for sweep_index in range(ITERS):
        mixed_sum = jnp.zeros((activations.shape[0], K), jnp.float32)
        for column in range(N_COL):
            partial_value = jnp.dot(activations[:, column * quarter:(column + 1) * quarter].astype(jnp.float32), basis_now[column * quarter:(column + 1) * quarter].astype(jnp.float32), preferred_element_type=jnp.float32)
            rounded = lax.optimization_barrier(partial_value.astype(jnp.bfloat16))
            mixed_sum = mixed_sum + rounded.astype(jnp.float32)
        token_mix = mixed_sum.astype(jnp.bfloat16)
        moment = contract_rows(activations, token_mix) * (1.0 / TOKENS)
        gram_sum = lax.dot_general(moment.astype(jnp.float32), moment.astype(jnp.float32), (((0,), (0,)), ((), ())), precision=lax.Precision.HIGHEST, preferred_element_type=jnp.float32)
        factor_low = jnp.linalg.cholesky(gram_sum)
        solved = jax.scipy.linalg.solve_triangular(factor_low, moment.T, lower=True)
        basis_now = solved.T.astype(jnp.bfloat16)
    coefficients = contract_rows(basis_now, gradient).astype(jnp.bfloat16)
    removed = jnp.dot(basis_now.astype(jnp.float32), coefficients.astype(jnp.float32), preferred_element_type=jnp.float32)
    return (gradient.astype(jnp.float32) - removed).astype(jnp.bfloat16)
```

```python
import jax
import jax.numpy as jnp
from jax import lax
from jax.experimental import pallas as pl
from jax.experimental.pallas import tpu as pltpu
from jax.sharding import PartitionSpec as P

ITERS = 2
BLOCK = 128
ROWS = 8
F32 = jnp.float32
BF16 = jnp.bfloat16

def split3(value):
    high = value.astype(jnp.bfloat16).astype(jnp.float32)
    rest = value - high
    mid = rest.astype(jnp.bfloat16).astype(jnp.float32)
    return high, mid, rest - mid


def panel_update(lower, upper):
    a_high, a_mid, a_low = split3(lower)
    b_high, b_mid, b_low = split3(upper)
    left = jnp.concatenate([a_high, a_high, a_mid, a_mid, a_high, a_low], axis=0).astype(jnp.bfloat16)
    right = jnp.concatenate([b_high, b_mid, b_high, b_mid, b_low, b_high], axis=0).astype(jnp.bfloat16)
    return lax.dot_general(left, right, (((0,), (0,)), ((), ())), preferred_element_type=jnp.float32)


def eliminate(rows, start):
    row_id = lax.broadcasted_iota(jnp.int32, (ROWS, BLOCK), 0)
    block_rows, inverse_rows = rows
    columns = [jnp.broadcast_to(block_rows[:, start + j:start + j + 1], (ROWS, BLOCK)) for j in range(ROWS)]
    pivots = jnp.ones((ROWS, BLOCK), jnp.float32)
    for j in range(ROWS):
        pivot = jnp.broadcast_to(columns[j][j:j + 1], (ROWS, BLOCK))
        pivots = jnp.where(row_id == j, pivot, pivots)
        if j + 1 < ROWS:
            factor = jnp.where(row_id > j, columns[j] / pivot, 0.0)
            for k in range(j + 1, ROWS):
                columns[k] = columns[k] - factor * jnp.broadcast_to(columns[k][j:j + 1], (ROWS, BLOCK))
            block_rows = block_rows - factor * jnp.broadcast_to(block_rows[j:j + 1], (ROWS, BLOCK))
            inverse_rows = inverse_rows - factor * jnp.broadcast_to(inverse_rows[j:j + 1], (ROWS, BLOCK))
    scale = lax.rsqrt(pivots)
    return block_rows * scale, inverse_rows * scale


def hdot(a, b, dims):
    return lax.dot_general(a, b, (dims, ((), ())), precision=lax.Precision.HIGHEST, preferred_element_type=jnp.float32)


def factor_kernel(gram_ref, inverse_ref, schur, block, block_inv):
    size = gram_ref.shape[0]
    count = size // BLOCK
    schur[...] = gram_ref[...]
    inverse_ref[...] = jnp.zeros_like(inverse_ref)
    eye = (lax.broadcasted_iota(jnp.int32, (BLOCK, BLOCK), 0) == lax.broadcasted_iota(jnp.int32, (BLOCK, BLOCK), 1)).astype(jnp.float32)

    @pl.loop(0, count)
    def _(step):
        at = pl.ds(pl.multiple_of(step * BLOCK, BLOCK), BLOCK)
        block[...] = schur[at, at]
        block_inv[...] = eye
        for start in range(0, BLOCK, ROWS):
            part = slice(start, start + ROWS)
            upper, inv = eliminate((block[part, :], block_inv[part, :]), start)
            block_inv[part, :] = inv
            if start + ROWS < BLOCK:
                change = panel_update(upper, jnp.concatenate([upper, inv], axis=1))
                rest = slice(start + ROWS, BLOCK)
                block[rest, :] -= change[start + ROWS:, :BLOCK]
                block_inv[rest, :] -= change[start + ROWS:, BLOCK:]
        inv = block_inv[...]
        upper_row = hdot(inv, schur[at, :], ((1,), (0,)))
        inverse_row = hdot(inv, inverse_ref[at, :], ((1,), (0,)))
        inverse_ref[at, :] = inverse_row
        inverse_ref[at, at] = inv
        inverse_row = inverse_ref[at, :]
        for other in range(1, count):
            @pl.when(other > step)
            def _():
                rows = slice(other * BLOCK, (other + 1) * BLOCK)
                left = upper_row[:, rows]
                schur[rows, :] -= hdot(left, upper_row, ((0,), (0,)))
                inverse_ref[rows, :] -= hdot(left, inverse_row, ((0,), (0,)))


def inverse_factor(gram):
    size = gram.shape[0]
    return pl.pallas_call(
        factor_kernel,
        out_shape=jax.ShapeDtypeStruct((size, size), jnp.float32),
        in_specs=[pl.BlockSpec(memory_space=pltpu.VMEM)],
        out_specs=pl.BlockSpec(memory_space=pltpu.VMEM),
        scratch_shapes=[pltpu.VMEM((size, size), jnp.float32), pltpu.VMEM((BLOCK, BLOCK), jnp.float32), pltpu.VMEM((BLOCK, BLOCK), jnp.float32)],
        name="inverse_factor",
    )(gram)


def dot(left, right, contract, precision=None):
    return lax.dot_general(left, right, ((contract[:1], contract[1:]), ((), ())), precision=precision, preferred_element_type=F32)


def swap(value, axis, bit):
    count = lax.axis_size(axis)
    return lax.ppermute(value, axis, [(i, i ^ (1 << bit)) for i in range(count)])


def bits_of(axis):
    return (lax.axis_size(axis) - 1).bit_length()


def side(axis, bit):
    return (lax.axis_index(axis) >> bit) & 1


def halve(value, axis, bit):
    mine = side(axis, bit)
    halves = value.reshape(2, value.shape[0] // 2, value.shape[1])
    away = lax.dynamic_index_in_dim(halves, 1 - mine, 0, keepdims=False).astype(BF16)
    kept = lax.dynamic_index_in_dim(halves, mine, 0, keepdims=False)
    return kept.astype(F32) + swap(away, axis, bit).astype(F32)


def double(value, axis, bit, dimension=0):
    mine = side(axis, bit)
    other = swap(value, axis, bit)
    return jnp.where(mine == 0, jnp.concatenate([value, other], dimension), jnp.concatenate([other, value], dimension))


def exchange_sum(value, axis, bit):
    rounded = value.astype(BF16)
    return rounded.astype(F32) + swap(rounded, axis, bit).astype(F32)


def sum_columns(value):
    total = halve(value, "col", 0)
    for bit in range(1, bits_of("col")):
        total = exchange_sum(total, "col", bit)
    return double(total.astype(BF16), "col", 0)


def scatter_tokens(value, order):
    for bit in order:
        value = halve(value, "seq", bit)
    return value.astype(BF16)


def gather_tokens(value, order):
    for bit in reversed(order):
        value = double(value, "seq", bit)
    return value


def on_device(activations, start_basis, gradient):
    inv_count = 1.0 / (activations.shape[0] * lax.axis_size("seq"))
    size = start_basis.shape[1]
    half = size // 2
    bits = bits_of("seq")
    orders = (tuple(range(bits)), tuple(range(1, bits)) + (0,))
    basis = start_basis.T
    for sweep_index in range(ITERS):
        pieces = []
        for chunk, order in enumerate(orders):
            rows = basis[chunk * half:(chunk + 1) * half]
            mix = sum_columns(dot(activations, rows, (1, 1)))
            partial_moment = dot(mix, activations, (0, 0)) * inv_count
            pieces.append(gather_tokens(scatter_tokens(partial_moment, order), order))
        moment = jnp.concatenate(pieces, 0)
        gram = sum_columns(dot(moment, moment, (1, 1))).astype(F32)
        inverse = inverse_factor(gram)
        basis = dot(inverse, moment.astype(F32), (1, 0), lax.Precision.HIGH).astype(BF16)
    full_basis = basis
    for bit in range(bits_of("col")):
        full_basis = gather_columns(full_basis, bit)
    width = basis.shape[1]
    full_basis = full_basis.reshape(-1, size, width)
    full_basis = jnp.concatenate([full_basis[i] for i in range(full_basis.shape[0])], 1)
    coefficients = dot(full_basis, gradient, (1, 0)).astype(BF16)
    removed = dot(full_basis, coefficients, (0, 0))
    return (gradient.astype(F32) - removed).astype(BF16)


def gather_columns(value, bit):
    return double(value, "col", bit)


def solution(mesh):
    return jax.shard_map(
        on_device,
        mesh=mesh,
        in_specs=(P("seq", "col"), P("col", None), P(None, ("seq", "col"))),
        out_specs=P(None, ("seq", "col")),
        check_vma=False,
    )
```

```python
import jax
import jax.numpy as jnp
from jax import lax
from jax.experimental import pallas as pl
from jax.experimental.pallas import tpu as pltpu
from jax.sharding import PartitionSpec as P

ITERS = 2
BLOCK = 128
ROWS = 8
PANEL = 32
F32 = jnp.float32
BF16 = jnp.bfloat16

def split3(value):
    high = value.astype(jnp.bfloat16).astype(jnp.float32)
    rest = value - high
    mid = rest.astype(jnp.bfloat16).astype(jnp.float32)
    return high, mid, rest - mid


def panel_update(lower, upper):
    a_high, a_mid, a_low = split3(lower)
    b_high, b_mid, b_low = split3(upper)
    left = jnp.concatenate([a_high, a_high, a_mid, a_mid, a_high, a_low], axis=0).astype(jnp.bfloat16)
    right = jnp.concatenate([b_high, b_mid, b_high, b_mid, b_low, b_high], axis=0).astype(jnp.bfloat16)
    return lax.dot_general(left, right, (((0,), (0,)), ((), ())), preferred_element_type=jnp.float32)


def spread_lane(value, lane):
    index = jnp.full((ROWS, BLOCK), lane, jnp.int32)
    return jnp.take_along_axis(value, index, axis=1, mode="promise_in_bounds")


def spread_row(value, row):
    return jnp.broadcast_to(value[row:row + 1], (ROWS, BLOCK))


def eliminate(block_rows, inverse_rows, start):
    groups = len(block_rows)
    row_id = lax.broadcasted_iota(jnp.int32, (ROWS, BLOCK), 0)
    columns = [[spread_lane(block_rows[g], start + k) for k in range(ROWS * (g + 1))] for g in range(groups)]
    pivots = [jnp.ones((ROWS, BLOCK), jnp.float32) for _ in range(groups)]
    for j in range(ROWS * groups):
        home, row = divmod(j, ROWS)
        pivot = spread_row(columns[home][j], row)
        pivots[home] = jnp.where(row_id == row, pivot, pivots[home])
        inverse_pivot = 1.0 / pivot
        below = [spread_row(columns[k // ROWS][j], k % ROWS) for k in range(j + 1, ROWS * groups)]
        block_row, inverse_row = spread_row(block_rows[home], row), spread_row(inverse_rows[home], row)
        for g in range(home, groups):
            factor = columns[g][j] * inverse_pivot
            if g == home:
                factor = jnp.where(row_id > row, factor, 0.0)
            for k in range(j + 1, ROWS * (g + 1)):
                columns[g][k] = columns[g][k] - factor * below[k - j - 1]
            block_rows[g] = block_rows[g] - factor * block_row
            inverse_rows[g] = inverse_rows[g] - factor * inverse_row
    scale = [lax.rsqrt(p) for p in pivots]
    return (
        jnp.concatenate([b * s for b, s in zip(block_rows, scale)], axis=0),
        jnp.concatenate([b * s for b, s in zip(inverse_rows, scale)], axis=0),
    )


def hdot(a, b, dims):
    return lax.dot_general(a, b, (dims, ((), ())), precision=lax.Precision.HIGHEST, preferred_element_type=jnp.float32)


def factor_kernel(gram_ref, inverse_ref, schur, block, block_inv):
    size = gram_ref.shape[0]
    count = size // BLOCK
    schur[...] = gram_ref[...]
    inverse_ref[...] = jnp.zeros_like(inverse_ref)
    eye = (lax.broadcasted_iota(jnp.int32, (BLOCK, BLOCK), 0) == lax.broadcasted_iota(jnp.int32, (BLOCK, BLOCK), 1)).astype(jnp.float32)

    @pl.loop(0, count)
    def _(step):
        at = pl.ds(pl.multiple_of(step * BLOCK, BLOCK), BLOCK)
        block[...] = schur[at, at]
        block_inv[...] = eye
        for start in range(0, BLOCK, PANEL):
            parts = [slice(at_row, at_row + ROWS) for at_row in range(start, start + PANEL, ROWS)]
            upper, inv = eliminate([block[part, :] for part in parts], [block_inv[part, :] for part in parts], start)
            block_inv[start:start + PANEL, :] = inv
            if start + PANEL < BLOCK:
                change = panel_update(upper, jnp.concatenate([upper, inv], axis=1))
                rest = slice(start + PANEL, BLOCK)
                block[rest, :] -= change[start + PANEL:, :BLOCK]
                block_inv[rest, :] -= change[start + PANEL:, BLOCK:]
        inv = block_inv[...]
        upper_row = hdot(inv, schur[at, :], ((1,), (0,)))
        inverse_row = hdot(inv, inverse_ref[at, :], ((1,), (0,)))
        inverse_ref[at, :] = inverse_row
        inverse_ref[at, at] = inv
        inverse_row = inverse_ref[at, :]
        for other in range(1, count):
            @pl.when(other > step)
            def _():
                rows = slice(other * BLOCK, (other + 1) * BLOCK)
                left = upper_row[:, rows]
                schur[rows, :] -= hdot(left, upper_row, ((0,), (0,)))
                inverse_ref[rows, :] -= hdot(left, inverse_row, ((0,), (0,)))


def inverse_factor(gram):
    size = gram.shape[0]
    return pl.pallas_call(
        factor_kernel,
        out_shape=jax.ShapeDtypeStruct((size, size), jnp.float32),
        in_specs=[pl.BlockSpec(memory_space=pltpu.VMEM)],
        out_specs=pl.BlockSpec(memory_space=pltpu.VMEM),
        scratch_shapes=[pltpu.VMEM((size, size), jnp.float32), pltpu.VMEM((BLOCK, BLOCK), jnp.float32), pltpu.VMEM((BLOCK, BLOCK), jnp.float32)],
        name="inverse_factor",
    )(gram)


def dot(left, right, contract, precision=None):
    return lax.dot_general(left, right, ((contract[:1], contract[1:]), ((), ())), precision=precision, preferred_element_type=F32)


def split_dot(left, right, contract):
    high = left.astype(BF16)
    low = (left - high.astype(F32)).astype(BF16)
    return dot(high, right, contract) + dot(low, right, contract)


def swap(value, axis, bit):
    count = lax.axis_size(axis)
    return lax.ppermute(value, axis, [(i, i ^ (1 << bit)) for i in range(count)])


def bits_of(axis):
    return (lax.axis_size(axis) - 1).bit_length()


def side(axis, bit):
    return (lax.axis_index(axis) >> bit) & 1


def halve(value, axis, bit, held=BF16):
    mine = side(axis, bit)
    halves = value.reshape(2, value.shape[0] // 2, value.shape[1])
    away = lax.dynamic_index_in_dim(halves, 1 - mine, 0, keepdims=False).astype(held)
    kept = lax.dynamic_index_in_dim(halves, mine, 0, keepdims=False)
    return kept.astype(F32) + swap(away, axis, bit).astype(F32)


def double(value, axis, bit, dimension=0):
    mine = side(axis, bit)
    other = swap(value, axis, bit)
    return jnp.where(mine == 0, jnp.concatenate([value, other], dimension), jnp.concatenate([other, value], dimension))


def exchange_sum(value, axis, bit):
    rounded = value.astype(BF16)
    return rounded.astype(F32) + swap(rounded, axis, bit).astype(F32)


def sum_columns(value, held=BF16):
    total = halve(value, "col", 0, held)
    for bit in range(1, bits_of("col")):
        total = exchange_sum(total, "col", bit)
    return double(total.astype(held), "col", 0)


def sum_tokens(value, order):
    for bit in order[:-1]:
        value = halve(value, "seq", bit)
    value = exchange_sum(value, "seq", order[-1]).astype(BF16)
    for bit in reversed(order[:-1]):
        value = double(value, "seq", bit)
    return value


def on_device(activations, start_basis, gradient):
    inv_count = 1.0 / (activations.shape[0] * lax.axis_size("seq"))
    size = start_basis.shape[1]
    bits = bits_of("seq")
    orders = (tuple(range(bits)), tuple(range(1, bits)) + (0,))
    half = size // len(orders)

    def moment_of(mix, order):
        return sum_tokens(dot(mix, activations, (1, 0)) * inv_count, order)

    first, second = [], []
    for chunk, order in enumerate(orders):
        columns = start_basis[:, chunk * half:(chunk + 1) * half]
        first.append(moment_of(sum_columns(dot(columns, activations, (0, 1))), order))
    for part, order in zip(first, orders):
        second.append(moment_of(sum_columns(dot(part, activations, (1, 1))), order))
    first = jnp.concatenate(first, 0)
    inverse = inverse_factor(sum_columns(dot(first, first, (1, 1)), F32))
    second = jnp.concatenate(second, 0)
    moment = split_dot(inverse, second, (1, 0)).astype(BF16)
    inverse = inverse_factor(sum_columns(dot(moment, moment, (1, 1)), F32))
    full = moment
    for bit in reversed(range(bits_of("col"))):
        full = double(full, "col", bit, 1)
    blocks = [full[:, i * moment.shape[1]:(i + 1) * moment.shape[1]] for i in column_order()]
    full = jnp.concatenate(blocks, 1)
    products = dot(full, gradient, (1, 0))
    coefficients = dot(inverse, products, (1, 0), lax.Precision.HIGH).astype(BF16)
    weights = split_dot(inverse, coefficients, (0, 0)).astype(BF16)
    removed = dot(full, weights, (0, 0))
    return (gradient.astype(F32) - removed).astype(BF16)


def column_order():
    bits = bits_of("col")
    return [sum(((i >> bit) & 1) << (bits - 1 - bit) for bit in range(bits)) for i in range(1 << bits)]


def solution(mesh):
    return jax.shard_map(
        on_device,
        mesh=mesh,
        in_specs=(P("seq", "col"), P("col", None), P(None, ("seq", "col"))),
        out_specs=P(None, ("seq", "col")),
        check_vma=False,
    )
```
